128 devices in a mesh: segment: 4 (over x_lo, core), expert: 32 (over x_hi, z, y).
Axes of the slice: x: 4 (x_hi: 2, x_lo: 2; x = x_hi * 2 + x_lo), y: 4, z: 4, core: 2. Of those that a mesh axis runs over, the one named last changes fastest.
Arguments:
- inputs: bfloat16 [2, 2048, 2560], P(None, 'expert'), may hold values from -6 to 6
- cotangent: bfloat16 [2, 2048, 2560], P(None, 'expert'), may hold values from -6 to 6
- norm_gain: float32 [4, 2560], P('segment'), may hold values from 0.5 to 1.5
- routes: int32 [4, 2, 2048, 6], P('segment', None, 'expert'), may hold values from 0 to 31, all different within a row; in each aligned block of 64 rows (0 to 63, 64 to 127, ..., all dimensions but the last counted through in order) at most 16 rows name the same one
- route_gates: float32 [4, 2, 2048, 6], P('segment', None, 'expert'), may hold values from 0.05 to 1
- w_gate: bfloat16 [4, 32, 2560, 768], P('segment', 'expert'), may hold values from -0.125 to 0.125
- w_up: bfloat16 [4, 32, 2560, 768], P('segment', 'expert'), may hold values from -0.125 to 0.125
- w_down: bfloat16 [4, 32, 768, 2560], P('segment', 'expert'), may hold values from -0.21875 to 0.21875
Outputs:
- states: bfloat16 [4, 2, 2048, 2560], P('segment', None, 'expert')
- input_grads: bfloat16 [4, 2, 2048, 2560], P('segment', None, 'expert')
The draws below stay inside these ranges and needn't reach their ends.
Inputs may be any that keep to these rules, and one draw needn't show every extreme that they name: `routes`: within the 64 tokens of one device in one micro-batch and layer, no expert is named by more than 16 tokens, a bound that some block reaches; each token names 6 different experts.
All inputs are finite; a program needn't handle non-finite values.
Results may differ from the reference program's by a relative error of at most 0.024.
Values may be sent and summed in bfloat16 or wider, within the bound.
No kernel may reach another device: no remote copies, remote signals or barrier semaphores. Data moves between devices by JAX's collectives and lax.ppermute only.
A program may use at most 192 MiB of HBM per device.

```python
import math
import jax
import jax.numpy as jnp
import numpy as np
from jax import lax

D = 2560
H = 768
TOP = 6
MICRO = 2
TOK_MB = 64
LAYERS = 4
EXPERTS = 32
TOKENS = 2048
CAP = 16
N_EXPERT = 32


def steps_of(rng, dims, split, least, high):
    def one(axis_at, parts):
        steps = jax.random.uniform(jax.random.fold_in(jax.random.fold_in(rng, 6), axis_at), (parts,), jnp.float32, least / len(split), high / len(split))
        return jnp.repeat(jnp.exp(steps), dims[axis_at] // parts).reshape((-1,) + (1,) * (len(dims) - axis_at - 1))

    gain = one(*split[0])
    for cut in split[1:]:
        gain = gain * one(*cut)
    return gain


def routed_block(rng, own, number, rows, amount, top, most, slope):
    order = jax.random.permutation(rng, amount)
    packed, common = portions_of(amount, rows * top, most, slope, True), portions_of(amount, rows * top, most, slope, False)
    places = jnp.arange(amount)

    def named(lengths, turn):
        used = int((lengths > 0).sum())
        fixed = max(1, used // 4)
        shifted = fixed + (places - fixed + turn * (used - fixed)) % max(1, amount - fixed)
        return jnp.zeros((amount,), jnp.int32).at[order[jnp.where(places < fixed, places, shifted)]].set(jnp.asarray(lengths, jnp.int32))

    lengths = jnp.where(number % 4 == 0, named(packed, number // 4), named(common, number - number // 4 - 1))
    mixed = jax.random.permutation(jax.random.fold_in(own, 3), amount)
    source_of, receiver = mixed[0:amount // 2 * 2:2], mixed[1:amount // 2 * 2:2]
    margin = jnp.minimum(lengths[source_of] - 1, most - lengths[receiver]) // 2
    margin = jnp.where((source_of == order[0]) | (receiver == order[0]) | (lengths[receiver] == 0), 0, jnp.maximum(margin, 0))
    shifted = jax.random.randint(jax.random.fold_in(own, 4), (amount // 2,), 0, 1 << 20) % (margin + 1)
    lengths = lengths.at[source_of].add(-shifted).at[receiver].add(shifted)
    labels = jnp.searchsorted(jnp.cumsum(lengths), jnp.arange(rows * top), side="right").astype(jnp.int32)
    listing = labels.reshape(top, rows).T
    listing = listing[jax.random.permutation(jax.random.fold_in(own, 1), rows)]
    turn = jax.random.randint(jax.random.fold_in(own, 2), (rows, 1), 0, top)
    return jnp.take_along_axis(listing, (jnp.arange(top)[None, :] + turn) % top, axis=1)


def portions_of(number_of, total, bound, lean, full):
    loads = [(1 << 20) // math.isqrt(rank ** lean) + 1 for rank in range(1, number_of + 1)]
    largest = bound if full else min(bound, max(-(-total // number_of), total * loads[0] // sum(loads)))
    least = 1 if total - largest >= number_of - 1 else 0
    holding, rest = [largest] + [least] * (number_of - 1), total - largest - least * (number_of - 1)
    while rest > 0:
        movable = [i for i in range(1, number_of) if holding[i] < largest] or [i for i in range(1, number_of) if holding[i] < bound]
        mass, budget = sum([loads[i] for i in movable]), rest
        for i in movable:
            more = min(bound - holding[i], max(1, budget * loads[i] // mass), rest)
            holding[i] = holding[i] + more
            rest = rest - more
    return np.array(holding)


def noise(stream_key, dims, width, most, cuts=(), kind=jnp.bfloat16):
    values = width * jax.random.normal(stream_key, dims, jnp.float32)
    if cuts:
        values = values * steps_of(stream_key, dims, cuts, -0.22, 0.18)
    return jnp.clip(values, -most, most).astype(kind)


def setup_inputs(seed: int = 0) -> dict:
    key_list = jax.random.split(jax.random.key(seed), 9)
    inputs = noise(key_list[0], (MICRO, TOKENS, D), 1.0, 6.0, ((1, 32),))
    cotangent = noise(key_list[1], (MICRO, TOKENS, D), 1.0, 6.0, ((1, 32),))
    norm_gain = jnp.clip(1.0 + 0.1 * jax.random.normal(key_list[2], (LAYERS, D), jnp.float32), 0.5, 1.5)
    routes_keys = jax.random.split(jax.random.fold_in(key_list[3], 1), LAYERS * MICRO * TOKENS // TOK_MB)
    routes_turns = jax.random.permutation(jax.random.fold_in(key_list[3], 3), LAYERS * MICRO * TOKENS // TOK_MB)
    routes = jax.vmap(lambda own, number: routed_block(jax.random.fold_in(key_list[3], 2), own, number, TOK_MB, EXPERTS, TOP, CAP, 2))(routes_keys, routes_turns).reshape((LAYERS, MICRO, TOKENS, TOP))
    route_gates = jnp.clip(jnp.exp(math.log(1.0) - 2.9957323 * jax.random.uniform(key_list[4], (LAYERS, MICRO, TOKENS, TOP), jnp.float32) ** steps_of(key_list[4], (LAYERS, MICRO, TOKENS, TOP), ((0, 4), (2, 32)), -0.2, 0.2)), 0.05, 1.0)
    w_gate = noise(key_list[5], (LAYERS, EXPERTS, D, H), D ** -0.5, 0.125, ((0, 4), (1, 32)))
    w_up = noise(key_list[6], (LAYERS, EXPERTS, D, H), D ** -0.5, 0.125, ((0, 4), (1, 32)))
    w_down = noise(key_list[7], (LAYERS, EXPERTS, H, D), H ** -0.5, 0.21875, ((0, 4), (1, 32)))
    return dict(inputs=inputs, cotangent=cotangent, norm_gain=norm_gain, routes=routes, route_gates=route_gates, w_gate=w_gate, w_up=w_up, w_down=w_down)


epsilon = 1e-06

def slot_table(route_block, experts, capacity):
    flat_ids = route_block.reshape(-1).astype(jnp.int32)
    onehot = (flat_ids[:, None] == jnp.arange(experts, dtype=jnp.int32)[None, :]).astype(jnp.int32)
    before = jnp.cumsum(onehot, axis=0) - onehot
    position = lax.optimization_barrier(jnp.sum(before * onehot, axis=1)).astype(jnp.int32)
    return (flat_ids * capacity + position).astype(jnp.int32).reshape(route_block.shape)

def expert_forward(row_block, gate_mat, up_mat, down_mat):
    gate_pre = jnp.dot(row_block, gate_mat, preferred_element_type=jnp.float32)
    up_val = jnp.dot(row_block, up_mat, preferred_element_type=jnp.float32)
    activated = (jax.nn.silu(gate_pre) * up_val).astype(jnp.bfloat16)
    expert_out = jnp.dot(activated, down_mat, preferred_element_type=jnp.float32).astype(jnp.bfloat16)
    return (expert_out, gate_pre, up_val)

def expert_backward(d_out, gate_pre, up_val, gate_mat, up_mat, down_mat):
    contract = (((1,), (1,)), ((), ()))
    d_act = lax.dot_general(d_out, down_mat, contract, preferred_element_type=jnp.float32)
    sigmoid_g = jax.nn.sigmoid(gate_pre)
    d_gate = (d_act * up_val * sigmoid_g * (1.0 + gate_pre * (1.0 - sigmoid_g))).astype(jnp.bfloat16)
    d_up = (d_act * gate_pre * sigmoid_g).astype(jnp.bfloat16)
    summed = lax.dot_general(d_gate, gate_mat, contract, preferred_element_type=jnp.float32)
    summed = summed + lax.dot_general(d_up, up_mat, contract, preferred_element_type=jnp.float32)
    return summed.astype(jnp.bfloat16)

def global_slots(route_layer):
    blocks = route_layer.reshape(N_EXPERT, TOK_MB, TOP)
    return jax.vmap(lambda block_ids: slot_table(block_ids, EXPERTS, CAP))(blocks)

def source_ids(slot_ids):
    return jnp.broadcast_to(jnp.arange(N_EXPERT, dtype=jnp.int32)[:, None, None], slot_ids.shape)

def to_experts(spread_rows, slot_ids):
    buffer = jnp.zeros((N_EXPERT, EXPERTS * CAP, D), jnp.bfloat16)
    buffer = buffer.at[source_ids(slot_ids), slot_ids].set(spread_rows)
    buffer = buffer.reshape(N_EXPERT, EXPERTS, CAP, D).transpose(1, 0, 2, 3)
    return buffer.reshape(EXPERTS, N_EXPERT * CAP, D)

def from_experts(expert_rows, slot_ids):
    back_rows = expert_rows.reshape(EXPERTS, N_EXPERT, CAP, D).transpose(1, 0, 2, 3)
    back_rows = back_rows.reshape(N_EXPERT, EXPERTS * CAP, D)
    return back_rows[source_ids(slot_ids), slot_ids]

def forward_layer(layer_in, route_layer, gate_layer, gain_row, gate_mats, up_mats, down_mats):
    wide_in = layer_in.astype(jnp.float32)
    inv_rms = lax.rsqrt(lax.optimization_barrier(jnp.mean(wide_in * wide_in, axis=1, keepdims=True)) + epsilon)
    normed = (wide_in * inv_rms * gain_row).astype(jnp.bfloat16)
    slot_ids = global_slots(route_layer)
    spread = jnp.broadcast_to(normed.reshape(N_EXPERT, TOK_MB, 1, D), (N_EXPERT, TOK_MB, TOP, D))
    rows_all = to_experts(spread, slot_ids)

    def one_expert(pieces):
        return expert_forward(pieces[0], pieces[1], pieces[2], pieces[3])
    expert_out, gate_pre, up_val = lax.map(one_expert, (rows_all, gate_mats, up_mats, down_mats))
    picked = from_experts(expert_out, slot_ids).reshape(TOKENS, TOP, D)
    mixed_sum = lax.optimization_barrier(jnp.sum(gate_layer[:, :, None] * picked.astype(jnp.float32), axis=1))
    return ((wide_in + mixed_sum).astype(jnp.bfloat16), gate_pre, up_val)

def backward_layer(d_in, layer_in, route_layer, gate_layer, gain_row, gate_pre, up_val, gate_mats, up_mats, down_mats):
    wide_in = layer_in.astype(jnp.float32)
    inv_rms = lax.rsqrt(lax.optimization_barrier(jnp.mean(wide_in * wide_in, axis=1, keepdims=True)) + epsilon)
    d_wide = d_in.astype(jnp.float32)
    slot_ids = global_slots(route_layer)
    d_out = (gate_layer[:, :, None] * d_wide[:, None, :]).astype(jnp.bfloat16)
    rows_all = to_experts(d_out.reshape(N_EXPERT, TOK_MB, TOP, D), slot_ids)

    def one_expert(pieces):
        return expert_backward(pieces[0], pieces[1], pieces[2], pieces[3], pieces[4], pieces[5])
    d_rows = lax.map(one_expert, (rows_all, gate_pre, up_val, gate_mats, up_mats, down_mats))
    picked = from_experts(d_rows, slot_ids).reshape(TOKENS, TOP, D)
    d_norm = lax.optimization_barrier(jnp.sum(picked.astype(jnp.float32), axis=1))
    scaled = gain_row * d_norm
    inner = lax.optimization_barrier(jnp.mean(wide_in * scaled, axis=1, keepdims=True))
    cubed = inv_rms * inv_rms * inv_rms
    return (d_wide + inv_rms * scaled - wide_in * cubed * inner).astype(jnp.bfloat16)

def reference(inputs, cotangent, norm_gain, routes, route_gates, w_gate, w_up, w_down):
    state_list = []
    grad_list = []
    for micro_no in range(MICRO):
        layer_in = inputs[micro_no]
        kept_vals = []
        outs_here = []
        for layer_no in range(LAYERS):
            layer_out, gate_pre, up_val = forward_layer(layer_in, routes[layer_no, micro_no], route_gates[layer_no, micro_no], norm_gain[layer_no], w_gate[layer_no], w_up[layer_no], w_down[layer_no])
            kept_vals.append((layer_in, gate_pre, up_val))
            outs_here.append(layer_out)
            layer_in = layer_out
        d_in = cotangent[micro_no]
        grads_here = [None] * LAYERS
        for layer_no in reversed(range(LAYERS)):
            saved_in, gate_pre, up_val = kept_vals[layer_no]
            d_in = backward_layer(d_in, saved_in, routes[layer_no, micro_no], route_gates[layer_no, micro_no], norm_gain[layer_no], gate_pre, up_val, w_gate[layer_no], w_up[layer_no], w_down[layer_no])
            grads_here[layer_no] = d_in
        state_list.append(jnp.stack(outs_here))
        grad_list.append(jnp.stack(grads_here))
    return (jnp.stack(state_list, axis=1), jnp.stack(grad_list, axis=1))
```

```python
import jax
import jax.numpy as jnp
from jax import lax
from jax.sharding import PartitionSpec as P

TOP = 6

epsilon = 1e-06


def exchange(rows):
    feat = rows.shape[1]
    peers = lax.axis_size("expert")
    blocks = rows.reshape(peers, -1, feat)
    moved = lax.all_to_all(blocks, "expert", split_axis=0, concat_axis=0, tiled=True)
    return moved.reshape(rows.shape)


def slot_matrices(route_block, gate_block, experts, capacity):
    flat_ids = route_block.reshape(-1)
    count = flat_ids.shape[0]
    onehot = flat_ids[:, None] == jnp.arange(experts, dtype=jnp.int32)[None, :]
    order = jnp.arange(count, dtype=jnp.int32)
    earlier = (order[:, None] > order[None, :]).astype(jnp.bfloat16)
    before = jnp.dot(
        earlier, onehot.astype(jnp.bfloat16), preferred_element_type=jnp.float32
    )
    position = jnp.sum(jnp.where(onehot, before, 0.0), axis=1).astype(jnp.int32)
    slots = (flat_ids * capacity + position).reshape(route_block.shape)
    places = jnp.arange(experts * capacity, dtype=jnp.int32)
    hit = slots[:, :, None] == places[None, None, :]
    picks = jnp.sum(hit.astype(jnp.float32), axis=1)
    weights = jnp.sum(jnp.where(hit, gate_block[:, :, None], 0.0), axis=1)
    return picks.astype(jnp.bfloat16), weights


def spread(picks, rows):
    return lax.dot_general(
        picks, rows, (((0,), (0,)), ((), ())), preferred_element_type=jnp.float32
    )


def gathered_sum(weights, rows):
    high = lax.reduce_precision(weights, 8, 7)
    both = jnp.concatenate([high, weights - high], axis=0).astype(jnp.bfloat16)
    parts = jnp.dot(both, rows, preferred_element_type=jnp.float32)
    half = weights.shape[0]
    return parts[:half] + parts[half:]


def inverse_rms(wide_in):
    return lax.rsqrt(jnp.mean(wide_in * wide_in, axis=1, keepdims=True) + epsilon)


def normed_rows(layer_in, gain):
    wide_in = layer_in.astype(jnp.float32)
    return (wide_in * inverse_rms(wide_in) * gain).astype(jnp.bfloat16)


def hidden_forward(rows, gate_mat, up_mat):
    gate_pre = jnp.dot(rows, gate_mat, preferred_element_type=jnp.float32)
    up_val = jnp.dot(rows, up_mat, preferred_element_type=jnp.float32)
    activated = (jax.nn.silu(gate_pre) * up_val).astype(jnp.bfloat16)
    return activated, gate_pre, up_val


def project_down(activated, down_mat):
    return jnp.dot(activated, down_mat, preferred_element_type=jnp.float32).astype(jnp.bfloat16)


CONTRACT = (((1,), (1,)), ((), ()))


def hidden_grad(d_rows, down_mat):
    return lax.dot_general(d_rows, down_mat, CONTRACT, preferred_element_type=jnp.float32)


def rows_grad(d_act, gate_pre, up_val, gate_mat, up_mat):
    sigmoid_g = jax.nn.sigmoid(gate_pre)
    d_gate = (d_act * up_val * sigmoid_g * (1.0 + gate_pre * (1.0 - sigmoid_g))).astype(
        jnp.bfloat16
    )
    d_up = (d_act * gate_pre * sigmoid_g).astype(jnp.bfloat16)
    summed = lax.dot_general(d_gate, gate_mat, CONTRACT, preferred_element_type=jnp.float32)
    summed = summed + lax.dot_general(d_up, up_mat, CONTRACT, preferred_element_type=jnp.float32)
    return summed.astype(jnp.bfloat16)


def layer_grad(dy, layer_in, gain, picks, returned):
    wide_in = layer_in.astype(jnp.float32)
    inv_rms = inverse_rms(wide_in)
    d_norm = jnp.dot(picks, returned, preferred_element_type=jnp.float32)
    scaled = gain * d_norm
    inner = jnp.mean(wide_in * scaled, axis=1, keepdims=True)
    cubed = inv_rms * inv_rms * inv_rms
    return (dy.astype(jnp.float32) + inv_rms * scaled - wide_in * cubed * inner).astype(
        jnp.bfloat16
    )


def local(inputs, cotangent, norm_gain, routes, route_gates, w_gate, w_up, w_down):
    segment_id = lax.axis_index("segment")
    experts = lax.axis_size("expert") * w_gate.shape[1]
    micro_count, tok_rows, feat_width = inputs.shape
    capacity = min(tok_rows, 4 * tok_rows * TOP // (3 * experts))
    hidden = w_gate.shape[3]
    slots = experts * capacity
    mine = segment_id % 2
    early = segment_id < 2
    swap = [(0, 1), (1, 0), (2, 3), (3, 2)]

    def swapped(value):
        return lax.ppermute(value, "segment", swap)

    def ordered(own, other):
        low = jnp.where(mine == 0, own, other)
        high = jnp.where(mine == 0, other, own)
        return low, high

    def of_micro(value, which):
        return lax.dynamic_index_in_dim(value, which, 0, keepdims=False)

    own_mats = (w_gate[0, 0], w_up[0, 0], w_down[0, 0])
    route_low, route_high = ordered(
        of_micro(routes[0], mine), swapped(of_micro(routes[0], 1 - mine))
    )
    gate_low, gate_high = ordered(
        of_micro(route_gates[0], mine), swapped(of_micro(route_gates[0], 1 - mine))
    )
    gain_low, gain_high = ordered(norm_gain, swapped(norm_gain))
    other_mats = tuple(swapped(mat) for mat in own_mats)

    def with_mats(level, run, *values):
        return lax.cond(
            mine == level,
            lambda held: run(held, own_mats),
            lambda held: run(held, other_mats),
            values,
        )

    picks_low, mix_low = slot_matrices(route_low, gate_low, experts, capacity)
    picks_high, mix_high = slot_matrices(route_high, gate_high, experts, capacity)
    scale_low = jnp.sum(mix_low, axis=0)[:, None]
    scale_high = jnp.sum(mix_high, axis=0)[:, None]

    first_in = of_micro(inputs, mine)
    last_grad = of_micro(cotangent, mine)
    source = jnp.where(early, normed_rows(first_in, gain_low), last_grad)
    picks_first = jnp.where(early, picks_low, picks_high)
    scale_first = jnp.where(early, 1.0, scale_high)
    arrived = exchange((scale_first * spread(picks_first, source)).astype(jnp.bfloat16))

    def send_rows(layer_in, gain, picks):
        return exchange(spread(picks, normed_rows(layer_in, gain)).astype(jnp.bfloat16))

    def send_grads(dy, picks, scale):
        return exchange((scale * spread(picks, dy)).astype(jnp.bfloat16))

    def run_forward(held, mats):
        activated, gate_pre, up_val = hidden_forward(held[0], mats[0], mats[1])
        return project_down(activated, mats[2]), gate_pre, up_val

    def mixed(layer_in, mix, returned):
        return (layer_in.astype(jnp.float32) + gathered_sum(mix, returned)).astype(jnp.bfloat16)

    def run_backward(held, mats):
        d_rows, gate_pre, up_val = held
        return rows_grad(hidden_grad(d_rows, mats[2]), gate_pre, up_val, mats[0], mats[1])

    def run_joint(held, mats):
        rows, d_act = held
        activated, gate_pre, up_val = hidden_forward(rows, mats[0], mats[1])
        return activated, rows_grad(d_act, gate_pre, up_val, mats[0], mats[1])

    no_rows = jnp.zeros((tok_rows, feat_width), jnp.bfloat16)
    no_hidden = jnp.zeros((slots, hidden), jnp.float32)

    def climb(got):
        out_low, pre_low, up_low = with_mats(0, run_forward, got)
        state_low = mixed(first_in, mix_low, exchange(out_low))
        got_high = send_rows(state_low, gain_high, picks_high)
        out_high, pre_high, up_high = with_mats(1, run_forward, got_high)
        state_high = mixed(state_low, mix_high, exchange(out_high))
        return state_low, state_high, pre_low, up_low, pre_high, up_high

    def prepare(got):
        d_act = with_mats(1, lambda held, mats: hidden_grad(held[0], mats[2]), got)
        return no_rows, no_rows, d_act, no_hidden, no_hidden, no_hidden

    state_low, state_high, kept_a, kept_b, kept_c, kept_d = lax.cond(
        early, climb, prepare, arrived
    )
    relayed = lax.ppermute(state_high, "segment", [(0, 2), (1, 3)])

    def turn(held):
        layer_in, d_act = held
        got_low = send_rows(layer_in, gain_low, picks_low)
        out_low, pre_low, up_low = with_mats(0, run_forward, got_low)
        state = mixed(layer_in, mix_low, exchange(out_low))
        got_high = send_rows(state, gain_high, picks_high)
        activated, d_rows = with_mats(1, run_joint, got_high, d_act)
        grad_high = layer_grad(last_grad, state, gain_high, picks_high, exchange(d_rows))
        d_got = send_grads(grad_high, picks_low, scale_low)
        d_rows_low = with_mats(0, run_backward, d_got, pre_low, up_low)
        grad_low = layer_grad(grad_high, layer_in, gain_low, picks_low, exchange(d_rows_low))
        return state, activated, grad_high, grad_low

    def stay(held):
        return no_rows, jnp.zeros((slots, hidden), jnp.bfloat16), no_rows, no_rows

    turn_state, activated, turn_high, turn_low = lax.cond(early, stay, turn, (relayed, kept_a))
    came_back = lax.ppermute(turn_low, "segment", [(2, 0), (3, 1)])

    def descend(dy):
        d_got = send_grads(dy, picks_high, scale_high)
        d_rows_high = with_mats(1, run_backward, d_got, kept_c, kept_d)
        grad_high = layer_grad(dy, state_low, gain_high, picks_high, exchange(d_rows_high))
        d_got_low = send_grads(grad_high, picks_low, scale_low)
        d_rows_low = with_mats(0, run_backward, d_got_low, kept_a, kept_b)
        grad_low = layer_grad(grad_high, first_in, gain_low, picks_low, exchange(d_rows_low))
        return state_low, state_high, grad_low, grad_high

    def finish(dy):
        out_high = with_mats(1, lambda held, mats: project_down(held[0], mats[2]), activated)
        state = mixed(turn_state, mix_high, exchange(out_high))
        return turn_state, state, turn_low, turn_high

    end_low, end_high, back_low, back_high = lax.cond(early, descend, finish, came_back)
    kept = jnp.where(
        mine == 0, jnp.stack([end_low, back_low]), jnp.stack([end_high, back_high])
    )
    given = jnp.where(
        mine == 0, jnp.stack([end_high, back_high]), jnp.stack([end_low, back_low])
    )
    taken = swapped(given)
    first = jnp.where(mine == 0, kept, taken)
    second = jnp.where(mine == 0, taken, kept)
    return (
        jnp.stack([first[0], second[0]])[None],
        jnp.stack([first[1], second[1]])[None],
    )


def solution(mesh):
    placed = (
        P(None, "expert", None),
        P(None, "expert", None),
        P("segment", None),
        P("segment", None, "expert", None),
        P("segment", None, "expert", None),
        P("segment", "expert", None, None),
        P("segment", "expert", None, None),
        P("segment", "expert", None, None),
    )
    return jax.shard_map(
        local,
        mesh=mesh,
        in_specs=placed,
        out_specs=(P("segment", None, "expert", None), P("segment", None, "expert", None)),
        check_vma=False,
    )
```

```python
import jax
import jax.numpy as jnp
from jax import lax
from jax.experimental import pallas as pl
from jax.experimental.pallas import tpu as pltpu
from jax.sharding import PartitionSpec as P

TOP = 6

epsilon = 1e-06

LAG_NANOS = 20000
TURN_LAG_NANOS = 4000
RETURN_LAG_NANOS = 4000
AHEAD = 2
CONTRACT = (((1,), (1,)), ((), ()))
IN_HBM = pl.BlockSpec(memory_space=pl.ANY)
IN_SMEM = pl.BlockSpec(memory_space=pltpu.SMEM)
IN_VMEM = pl.BlockSpec(memory_space=pltpu.VMEM)


def late_kernel(nanos_ref, rows_ref, out_ref):
    pl.delay(nanos_ref[0])
    out_ref[...] = rows_ref[...]


def held_back(rows, nanos):
    return pl.pallas_call(
        late_kernel,
        out_shape=jax.ShapeDtypeStruct(rows.shape, rows.dtype),
        in_specs=[IN_SMEM, IN_VMEM],
        out_specs=IN_VMEM,
        name="held_back",
    )(nanos.reshape(1), rows)


def fetch(pick, own, other, target, sem):
    def start():
        @pl.when(pick == 0)
        def _():
            pltpu.make_async_copy(own, target, sem).start()

        @pl.when(pick != 0)
        def _():
            pltpu.make_async_copy(other, target, sem).start()

        return pltpu.make_async_copy(own, target, sem)

    return start


def brought(source, target, sem):
    return lambda: started(source, target, sem)


def started(source, target, sem):
    copy = pltpu.make_async_copy(source, target, sem)
    copy.start()
    return copy


def wait_all(copies):
    for copy in copies:
        copy.wait()


class Incoming:
    def __init__(self, starters):
        self.starters = starters
        self.flying = []
        self.taken = 0
        self.launch(1 + AHEAD)

    def launch(self, upto):
        for start in self.starters[len(self.flying) : upto]:
            self.flying.append(start())

    def take(self, count):
        for _ in range(count):
            self.flying[self.taken].wait()
            self.taken += 1
            self.launch(self.taken + 1 + AHEAD)


def pieces(total, widths):
    parts = []
    at = 0
    for width in widths:
        size = min(width, total - at)
        if size > 0:
            parts.append(pl.ds(at, size))
            at += size
    if at < total:
        parts.append(pl.ds(at, total - at))
    return parts


def hidden_pieces(total):
    return pieces(total, (256, 512))


def feature_pieces(total):
    return pieces(total, (1280, 768, 512))


def wide_dot(left, right):
    return jnp.dot(left, right, preferred_element_type=jnp.float32)


def turned_dot(left, right):
    return lax.dot_general(left, right, CONTRACT, preferred_element_type=jnp.float32)


def gate_grads(d_act, gate_pre, up_val):
    sigmoid_g = jax.nn.sigmoid(gate_pre)
    d_gate = d_act * up_val * sigmoid_g * (1.0 + gate_pre * (1.0 - sigmoid_g))
    d_up = d_act * gate_pre * sigmoid_g
    return d_gate.astype(jnp.bfloat16), d_up.astype(jnp.bfloat16)


def forward_kernel(
    pick_ref, rows_hbm, gate_a, up_a, down_a, gate_b, up_b, down_b,
    out_hbm, pre_hbm, val_hbm,
    rows, gate, up, down, pre, val, act, out, in_sem, gate_sem, up_sem, down_sem, pre_sem, val_sem, out_sem,
):
    pick = pick_ref[0]
    hidden_parts = hidden_pieces(gate.shape[1])
    feature_parts = feature_pieces(down.shape[1])
    line = [brought(rows_hbm, rows, in_sem)]
    for n, part in enumerate(hidden_parts):
        line.append(fetch(pick, gate_a.at[:, part], gate_b.at[:, part], gate.at[:, part], gate_sem.at[n]))
        line.append(fetch(pick, up_a.at[:, part], up_b.at[:, part], up.at[:, part], up_sem.at[n]))
    for n, part in enumerate(feature_parts):
        line.append(fetch(pick, down_a.at[:, part], down_b.at[:, part], down.at[:, part], down_sem.at[n]))
    incoming = Incoming(line)
    incoming.take(1)
    leaving = []
    for n, part in enumerate(hidden_parts):
        incoming.take(1)
        gate_pre = wide_dot(rows[...], gate[:, part])
        pre[:, part] = gate_pre
        incoming.take(1)
        up_val = wide_dot(rows[...], up[:, part])
        val[:, part] = up_val
        act[:, part] = (gate_pre * jax.nn.sigmoid(gate_pre) * up_val).astype(jnp.bfloat16)
        leaving.append(started(pre.at[:, part], pre_hbm.at[:, part], pre_sem.at[n]))
        leaving.append(started(val.at[:, part], val_hbm.at[:, part], val_sem.at[n]))
    for n, part in enumerate(feature_parts):
        incoming.take(1)
        out[:, part] = wide_dot(act[...], down[:, part]).astype(jnp.bfloat16)
        leaving.append(started(out.at[:, part], out_hbm.at[:, part], out_sem.at[n]))
    wait_all(leaving)


def expert_forward(pick, rows, own, other):
    slots, feat = rows.shape
    hidden = own[0].shape[1]
    count = len(hidden_pieces(hidden))
    wide = len(feature_pieces(feat))
    bf16, f32 = jnp.bfloat16, jnp.float32
    return pl.pallas_call(
        forward_kernel,
        out_shape=(
            jax.ShapeDtypeStruct((slots, feat), bf16),
            jax.ShapeDtypeStruct((slots, hidden), f32),
            jax.ShapeDtypeStruct((slots, hidden), f32),
        ),
        in_specs=[IN_SMEM] + [IN_HBM] * 7,
        out_specs=(IN_HBM,) * 3,
        scratch_shapes=[
            pltpu.VMEM((slots, feat), bf16),
            pltpu.VMEM((feat, hidden), bf16),
            pltpu.VMEM((feat, hidden), bf16),
            pltpu.VMEM((hidden, feat), bf16),
            pltpu.VMEM((slots, hidden), f32),
            pltpu.VMEM((slots, hidden), f32),
            pltpu.VMEM((slots, hidden), bf16),
            pltpu.VMEM((slots, feat), bf16),
            pltpu.SemaphoreType.DMA(()),
            pltpu.SemaphoreType.DMA((count,)),
            pltpu.SemaphoreType.DMA((count,)),
            pltpu.SemaphoreType.DMA((wide,)),
            pltpu.SemaphoreType.DMA((count,)),
            pltpu.SemaphoreType.DMA((count,)),
            pltpu.SemaphoreType.DMA((wide,)),
        ],
        name="expert_forward",
    )(pick.reshape(1), rows, *own, *other)


def backward_kernel(
    pick_ref, rows_hbm, pre_hbm, val_hbm, gate_a, up_a, down_a, gate_b, up_b, down_b,
    out_hbm,
    rows, gate, up, down, pre, val, d_gate, d_up, out, in_sem, gate_sem, up_sem, down_sem, pre_sem, val_sem, out_sem,
):
    pick = pick_ref[0]
    hidden_parts = hidden_pieces(gate.shape[1])
    feature_parts = feature_pieces(down.shape[1])
    line = [brought(rows_hbm, rows, in_sem)]
    for n, part in enumerate(hidden_parts):
        line.append(fetch(pick, down_a.at[part, :], down_b.at[part, :], down.at[part, :], down_sem.at[n]))
        line.append(brought(pre_hbm.at[:, part], pre.at[:, part], pre_sem.at[n]))
        line.append(brought(val_hbm.at[:, part], val.at[:, part], val_sem.at[n]))
    for n, part in enumerate(feature_parts):
        line.append(fetch(pick, gate_a.at[part, :], gate_b.at[part, :], gate.at[part, :], gate_sem.at[n]))
        line.append(fetch(pick, up_a.at[part, :], up_b.at[part, :], up.at[part, :], up_sem.at[n]))
    incoming = Incoming(line)
    incoming.take(1)
    for part in hidden_parts:
        incoming.take(1)
        d_act = turned_dot(rows[...], down[part, :])
        incoming.take(2)
        part_gate, part_up = gate_grads(d_act, pre[:, part], val[:, part])
        d_gate[:, part] = part_gate
        d_up[:, part] = part_up
    leaving = []
    for n, part in enumerate(feature_parts):
        incoming.take(2)
        summed = turned_dot(d_gate[...], gate[part, :]) + turned_dot(d_up[...], up[part, :])
        out[:, part] = summed.astype(jnp.bfloat16)
        leaving.append(started(out.at[:, part], out_hbm.at[:, part], out_sem.at[n]))
    wait_all(leaving)


def expert_backward(pick, rows, pre, val, own, other):
    slots, feat = rows.shape
    hidden = own[0].shape[1]
    count = len(hidden_pieces(hidden))
    wide = len(feature_pieces(feat))
    bf16, f32 = jnp.bfloat16, jnp.float32
    return pl.pallas_call(
        backward_kernel,
        out_shape=jax.ShapeDtypeStruct((slots, feat), bf16),
        in_specs=[IN_SMEM] + [IN_HBM] * 9,
        out_specs=IN_HBM,
        scratch_shapes=[
            pltpu.VMEM((slots, feat), bf16),
            pltpu.VMEM((feat, hidden), bf16),
            pltpu.VMEM((feat, hidden), bf16),
            pltpu.VMEM((hidden, feat), bf16),
            pltpu.VMEM((slots, hidden), f32),
            pltpu.VMEM((slots, hidden), f32),
            pltpu.VMEM((slots, hidden), bf16),
            pltpu.VMEM((slots, hidden), bf16),
            pltpu.VMEM((slots, feat), bf16),
            pltpu.SemaphoreType.DMA(()),
            pltpu.SemaphoreType.DMA((wide,)),
            pltpu.SemaphoreType.DMA((wide,)),
            pltpu.SemaphoreType.DMA((count,)),
            pltpu.SemaphoreType.DMA((count,)),
            pltpu.SemaphoreType.DMA((count,)),
            pltpu.SemaphoreType.DMA((wide,)),
        ],
        name="expert_backward",
    )(pick.reshape(1), rows, pre, val, *own, *other)


def joint_kernel(
    pick_ref, rows_hbm, d_act_hbm, gate_a, up_a, gate_b, up_b,
    act_hbm, out_hbm,
    rows, gate, up, d_act, act, d_gate, d_up, out, in_sem, gate_sem, up_sem, d_act_sem, act_sem, out_sem,
):
    pick = pick_ref[0]
    hidden_parts = hidden_pieces(gate.shape[1])
    feature_parts = feature_pieces(out.shape[1])
    line = [brought(rows_hbm, rows, in_sem)]
    for n, part in enumerate(hidden_parts):
        line.append(fetch(pick, gate_a.at[:, part], gate_b.at[:, part], gate.at[:, part], gate_sem.at[n]))
        line.append(fetch(pick, up_a.at[:, part], up_b.at[:, part], up.at[:, part], up_sem.at[n]))
        line.append(brought(d_act_hbm.at[:, part], d_act.at[:, part], d_act_sem.at[n]))
    incoming = Incoming(line)
    incoming.take(1)
    leaving = []
    for n, part in enumerate(hidden_parts):
        incoming.take(1)
        gate_pre = wide_dot(rows[...], gate[:, part])
        incoming.take(1)
        up_val = wide_dot(rows[...], up[:, part])
        act[:, part] = (gate_pre * jax.nn.sigmoid(gate_pre) * up_val).astype(jnp.bfloat16)
        leaving.append(started(act.at[:, part], act_hbm.at[:, part], act_sem.at[n]))
        incoming.take(1)
        part_gate, part_up = gate_grads(d_act[:, part], gate_pre, up_val)
        d_gate[:, part] = part_gate
        d_up[:, part] = part_up
    for n, part in enumerate(feature_parts):
        summed = turned_dot(d_gate[...], gate[part, :]) + turned_dot(d_up[...], up[part, :])
        out[:, part] = summed.astype(jnp.bfloat16)
        leaving.append(started(out.at[:, part], out_hbm.at[:, part], out_sem.at[n]))
    wait_all(leaving)


def expert_joint(pick, rows, d_act, own, other):
    slots, feat = rows.shape
    hidden = own[0].shape[1]
    count = len(hidden_pieces(hidden))
    wide = len(feature_pieces(feat))
    bf16, f32 = jnp.bfloat16, jnp.float32
    return pl.pallas_call(
        joint_kernel,
        out_shape=(
            jax.ShapeDtypeStruct((slots, hidden), bf16),
            jax.ShapeDtypeStruct((slots, feat), bf16),
        ),
        in_specs=[IN_SMEM] + [IN_HBM] * 6,
        out_specs=(IN_HBM,) * 2,
        scratch_shapes=[
            pltpu.VMEM((slots, feat), bf16),
            pltpu.VMEM((feat, hidden), bf16),
            pltpu.VMEM((feat, hidden), bf16),
            pltpu.VMEM((slots, hidden), f32),
            pltpu.VMEM((slots, hidden), bf16),
            pltpu.VMEM((slots, hidden), bf16),
            pltpu.VMEM((slots, hidden), bf16),
            pltpu.VMEM((slots, feat), bf16),
            pltpu.SemaphoreType.DMA(()),
            pltpu.SemaphoreType.DMA((count,)),
            pltpu.SemaphoreType.DMA((count,)),
            pltpu.SemaphoreType.DMA((count,)),
            pltpu.SemaphoreType.DMA((count,)),
            pltpu.SemaphoreType.DMA((wide,)),
        ],
        name="expert_joint",
    )(pick.reshape(1), rows, d_act, *own[:2], *other[:2])


def exchange(rows):
    feat = rows.shape[1]
    peers = lax.axis_size("expert")
    blocks = rows.reshape(peers, -1, feat)
    moved = lax.all_to_all(blocks, "expert", split_axis=0, concat_axis=0, tiled=True)
    return moved.reshape(rows.shape)


def slot_matrices(route_block, gate_block, experts, capacity):
    flat_ids = route_block.reshape(-1)
    count = flat_ids.shape[0]
    onehot = flat_ids[:, None] == jnp.arange(experts, dtype=jnp.int32)[None, :]
    order = jnp.arange(count, dtype=jnp.int32)
    earlier = (order[:, None] > order[None, :]).astype(jnp.bfloat16)
    before = jnp.dot(
        earlier, onehot.astype(jnp.bfloat16), preferred_element_type=jnp.float32
    )
    position = jnp.sum(jnp.where(onehot, before, 0.0), axis=1).astype(jnp.int32)
    slots = (flat_ids * capacity + position).reshape(route_block.shape)
    places = jnp.arange(experts * capacity, dtype=jnp.int32)
    hit = slots[:, :, None] == places[None, None, :]
    picks = jnp.sum(hit.astype(jnp.float32), axis=1)
    weights = jnp.sum(jnp.where(hit, gate_block[:, :, None], 0.0), axis=1)
    return picks.astype(jnp.bfloat16), weights


def spread(picks, rows):
    return lax.dot_general(
        picks, rows, (((0,), (0,)), ((), ())), preferred_element_type=jnp.float32
    )


def gathered_sum(weights, rows):
    high = lax.reduce_precision(weights, 8, 7)
    both = jnp.concatenate([high, weights - high], axis=0).astype(jnp.bfloat16)
    parts = jnp.dot(both, rows, preferred_element_type=jnp.float32)
    half = weights.shape[0]
    return parts[:half] + parts[half:]


def inverse_rms(wide_in):
    return lax.rsqrt(jnp.mean(wide_in * wide_in, axis=1, keepdims=True) + epsilon)


def normed_rows(layer_in, gain):
    wide_in = layer_in.astype(jnp.float32)
    return (wide_in * inverse_rms(wide_in) * gain).astype(jnp.bfloat16)


def project_down(activated, down_mat):
    return jnp.dot(activated, down_mat, preferred_element_type=jnp.float32).astype(jnp.bfloat16)


def hidden_grad(d_rows, down_mat):
    return lax.dot_general(d_rows, down_mat, CONTRACT, preferred_element_type=jnp.float32)


def layer_grad(dy, layer_in, gain, picks, returned):
    wide_in = layer_in.astype(jnp.float32)
    inv_rms = inverse_rms(wide_in)
    d_norm = jnp.dot(picks, returned, preferred_element_type=jnp.float32)
    scaled = gain * d_norm
    inner = jnp.mean(wide_in * scaled, axis=1, keepdims=True)
    cubed = inv_rms * inv_rms * inv_rms
    return (dy.astype(jnp.float32) + inv_rms * scaled - wide_in * cubed * inner).astype(
        jnp.bfloat16
    )


def local(inputs, cotangent, norm_gain, routes, route_gates, w_gate, w_up, w_down):
    segment_id = lax.axis_index("segment")
    experts = lax.axis_size("expert") * w_gate.shape[1]
    micro_count, tok_rows, feat_width = inputs.shape
    capacity = min(tok_rows, 4 * tok_rows * TOP // (3 * experts))
    hidden = w_gate.shape[3]
    slots = experts * capacity
    mine = segment_id % 2
    early = segment_id < 2
    swap = [(0, 1), (1, 0), (2, 3), (3, 2)]

    def swapped(value):
        return lax.ppermute(value, "segment", swap)

    def ordered(own, other):
        low = jnp.where(mine == 0, own, other)
        high = jnp.where(mine == 0, other, own)
        return low, high

    def of_micro(value, which):
        return lax.dynamic_index_in_dim(value, which, 0, keepdims=False)

    own_mats = (w_gate[0, 0], w_up[0, 0], w_down[0, 0])
    route_low, route_high = ordered(
        of_micro(routes[0], mine), swapped(of_micro(routes[0], 1 - mine))
    )
    gate_low, gate_high = ordered(
        of_micro(route_gates[0], mine), swapped(of_micro(route_gates[0], 1 - mine))
    )
    gain_low, gain_high = ordered(norm_gain, swapped(norm_gain))
    other_mats = tuple(swapped(mat) for mat in own_mats)

    def with_mats(level, run, *values):
        return lax.cond(
            mine == level,
            lambda held: run(held, own_mats),
            lambda held: run(held, other_mats),
            values,
        )

    low_pick = mine.astype(jnp.int32)
    high_pick = 1 - low_pick

    picks_low, mix_low = slot_matrices(route_low, gate_low, experts, capacity)
    picks_high, mix_high = slot_matrices(route_high, gate_high, experts, capacity)
    scale_low = jnp.sum(mix_low, axis=0)[:, None]
    scale_high = jnp.sum(mix_high, axis=0)[:, None]

    first_in = of_micro(inputs, mine)
    last_grad = of_micro(cotangent, mine)
    source = jnp.where(early, normed_rows(first_in, gain_low), last_grad)
    source = held_back(source, jnp.where(mine == 1, LAG_NANOS, 0).astype(jnp.int32))
    picks_first = jnp.where(early, picks_low, picks_high)
    scale_first = jnp.where(early, 1.0, scale_high)
    arrived = exchange((scale_first * spread(picks_first, source)).astype(jnp.bfloat16))

    def send_rows(layer_in, gain, picks):
        return exchange(spread(picks, normed_rows(layer_in, gain)).astype(jnp.bfloat16))

    def send_grads(dy, picks, scale):
        return exchange((scale * spread(picks, dy)).astype(jnp.bfloat16))

    def mixed(layer_in, mix, returned):
        return (layer_in.astype(jnp.float32) + gathered_sum(mix, returned)).astype(jnp.bfloat16)

    no_rows = jnp.zeros((tok_rows, feat_width), jnp.bfloat16)
    no_hidden = jnp.zeros((slots, hidden), jnp.float32)

    def climb(got):
        out_low, pre_low, up_low = expert_forward(low_pick, got, own_mats, other_mats)
        state_low = mixed(first_in, mix_low, exchange(out_low))
        got_high = send_rows(state_low, gain_high, picks_high)
        out_high, pre_high, up_high = expert_forward(high_pick, got_high, own_mats, other_mats)
        state_high = mixed(state_low, mix_high, exchange(out_high))
        return state_low, state_high, pre_low, up_low, pre_high, up_high

    def prepare(got):
        d_act = with_mats(1, lambda held, mats: hidden_grad(held[0], mats[2]), got)
        return no_rows, no_rows, d_act, no_hidden, no_hidden, no_hidden

    state_low, state_high, kept_a, kept_b, kept_c, kept_d = lax.cond(
        early, climb, prepare, arrived
    )
    relayed = lax.ppermute(state_high, "segment", [(0, 2), (1, 3)])

    relayed = held_back(relayed, jnp.where(mine == 1, TURN_LAG_NANOS, 0).astype(jnp.int32))

    def turn(held):
        layer_in, d_act = held
        got_low = send_rows(layer_in, gain_low, picks_low)
        out_low, pre_low, up_low = expert_forward(low_pick, got_low, own_mats, other_mats)
        state = mixed(layer_in, mix_low, exchange(out_low))
        got_high = send_rows(state, gain_high, picks_high)
        activated, d_rows = expert_joint(high_pick, got_high, d_act, own_mats, other_mats)
        grad_high = layer_grad(last_grad, state, gain_high, picks_high, exchange(d_rows))
        d_got = send_grads(grad_high, picks_low, scale_low)
        d_rows_low = expert_backward(low_pick, d_got, pre_low, up_low, own_mats, other_mats)
        grad_low = layer_grad(grad_high, layer_in, gain_low, picks_low, exchange(d_rows_low))
        return state, activated, grad_high, grad_low

    def stay(held):
        return no_rows, jnp.zeros((slots, hidden), jnp.bfloat16), no_rows, no_rows

    turn_state, activated, turn_high, turn_low = lax.cond(early, stay, turn, (relayed, kept_a))
    came_back = lax.ppermute(turn_low, "segment", [(2, 0), (3, 1)])

    came_back = held_back(came_back, jnp.where(mine == 1, RETURN_LAG_NANOS, 0).astype(jnp.int32))

    def descend(dy):
        d_got = send_grads(dy, picks_high, scale_high)
        d_rows_high = expert_backward(high_pick, d_got, kept_c, kept_d, own_mats, other_mats)
        grad_high = layer_grad(dy, state_low, gain_high, picks_high, exchange(d_rows_high))
        d_got_low = send_grads(grad_high, picks_low, scale_low)
        d_rows_low = expert_backward(low_pick, d_got_low, kept_a, kept_b, own_mats, other_mats)
        grad_low = layer_grad(grad_high, first_in, gain_low, picks_low, exchange(d_rows_low))
        return state_low, state_high, grad_low, grad_high

    def finish(dy):
        out_high = with_mats(1, lambda held, mats: project_down(held[0], mats[2]), activated)
        state = mixed(turn_state, mix_high, exchange(out_high))
        return turn_state, state, turn_low, turn_high

    end_low, end_high, back_low, back_high = lax.cond(early, descend, finish, came_back)
    kept = jnp.where(
        mine == 0, jnp.stack([end_low, back_low]), jnp.stack([end_high, back_high])
    )
    given = jnp.where(
        mine == 0, jnp.stack([end_high, back_high]), jnp.stack([end_low, back_low])
    )
    taken = swapped(given)
    first = jnp.where(mine == 0, kept, taken)
    second = jnp.where(mine == 0, taken, kept)
    return (
        jnp.stack([first[0], second[0]])[None],
        jnp.stack([first[1], second[1]])[None],
    )


def solution(mesh):
    placed = (
        P(None, "expert", None),
        P(None, "expert", None),
        P("segment", None),
        P("segment", None, "expert", None),
        P("segment", None, "expert", None),
        P("segment", "expert", None, None),
        P("segment", "expert", None, None),
        P("segment", "expert", None, None),
    )
    return jax.shard_map(
        local,
        mesh=mesh,
        in_specs=placed,
        out_specs=(P("segment", None, "expert", None), P("segment", None, "expert", None)),
        check_vma=False,
    )
```

```python
import jax
import jax.numpy as jnp
from jax import lax
from jax.experimental import pallas as pl
from jax.experimental.pallas import tpu as pltpu
from jax.sharding import PartitionSpec as P

TOP = 6

epsilon = 1e-06

LAG_NANOS = 20000
TURN_LAG_NANOS = 4000
RETURN_LAG_NANOS = 4000
FORWARD_AHEAD = 5
BACKWARD_AHEAD = 3
CONTRACT = (((1,), (1,)), ((), ()))
IN_HBM = pl.BlockSpec(memory_space=pl.ANY)
IN_SMEM = pl.BlockSpec(memory_space=pltpu.SMEM)
IN_VMEM = pl.BlockSpec(memory_space=pltpu.VMEM)


def late_kernel(nanos_ref, anchor_ref, value_ref, out_ref):
    pl.delay(nanos_ref[0])
    out_ref[...] = value_ref[...]


def held_back(anchor, value, nanos):
    return pl.pallas_call(
        late_kernel,
        out_shape=jax.ShapeDtypeStruct(value.shape, value.dtype),
        in_specs=[IN_SMEM, IN_HBM, IN_VMEM],
        out_specs=IN_VMEM,
        name="held_back",
    )(nanos.reshape(1), anchor, value)


def fetch(pick, own, other, target, sem):
    def start():
        @pl.when(pick == 0)
        def _():
            pltpu.make_async_copy(own, target, sem).start()

        @pl.when(pick != 0)
        def _():
            pltpu.make_async_copy(other, target, sem).start()

        return pltpu.make_async_copy(own, target, sem)

    return start


def brought(source, target, sem):
    return lambda: started(source, target, sem)


def started(source, target, sem):
    copy = pltpu.make_async_copy(source, target, sem)
    copy.start()
    return copy


def wait_all(copies):
    for copy in copies:
        copy.wait()


class Incoming:
    def __init__(self, starters, ahead):
        self.starters = starters
        self.ahead = ahead
        self.flying = []
        self.taken = 0
        self.launch(1 + ahead)

    def launch(self, upto):
        for start in self.starters[len(self.flying) : upto]:
            self.flying.append(start())

    def take(self, count):
        for _ in range(count):
            self.flying[self.taken].wait()
            self.taken += 1
            self.launch(self.taken + 1 + self.ahead)


def pieces(total, widths):
    parts = []
    at = 0
    for width in widths:
        size = min(width, total - at)
        if size > 0:
            parts.append(pl.ds(at, size))
            at += size
    if at < total:
        parts.append(pl.ds(at, total - at))
    return parts


def feature_pieces(total):
    return pieces(total, (512,) * (total // 512))


def wide_dot(left, right):
    return jnp.dot(left, right, preferred_element_type=jnp.float32)


def turned_dot(left, right):
    return lax.dot_general(left, right, CONTRACT, preferred_element_type=jnp.float32)


def gate_grads(d_act, gate_pre, up_val):
    sigmoid_g = jax.nn.sigmoid(gate_pre)
    d_gate = d_act * up_val * sigmoid_g * (1.0 + gate_pre * (1.0 - sigmoid_g))
    d_up = d_act * gate_pre * sigmoid_g
    return d_gate.astype(jnp.bfloat16), d_up.astype(jnp.bfloat16)


def forward_kernel(
    pick_ref, rows_hbm, gate_a, up_a, down_a, gate_b, up_b, down_b,
    out_hbm, pre_hbm, val_hbm,
    rows, gate, up, down, pre, val, act, out, in_sem, gate_sem, up_sem, down_sem, pre_sem, val_sem, out_sem,
):
    pick = pick_ref[0]
    feature_parts = feature_pieces(down.shape[1])
    line = []
    for n, part in enumerate(feature_parts):
        line.append(brought(rows_hbm.at[:, part], rows.at[:, part], in_sem.at[n]))
        line.append(fetch(pick, gate_a.at[part, :], gate_b.at[part, :], gate.at[part, :], gate_sem.at[n]))
        line.append(fetch(pick, up_a.at[part, :], up_b.at[part, :], up.at[part, :], up_sem.at[n]))
    for n, part in enumerate(feature_parts):
        line.append(fetch(pick, down_a.at[:, part], down_b.at[:, part], down.at[:, part], down_sem.at[n]))
    incoming = Incoming(line, FORWARD_AHEAD)
    for n, part in enumerate(feature_parts):
        incoming.take(3)
        gate_part = wide_dot(rows[:, part], gate[part, :])
        up_part = wide_dot(rows[:, part], up[part, :])
        pre[...] = gate_part if n == 0 else pre[...] + gate_part
        val[...] = up_part if n == 0 else val[...] + up_part
    leaving = [started(pre, pre_hbm, pre_sem), started(val, val_hbm, val_sem)]
    act[...] = (pre[...] * jax.nn.sigmoid(pre[...]) * val[...]).astype(jnp.bfloat16)
    for n, part in enumerate(feature_parts):
        incoming.take(1)
        out[:, part] = wide_dot(act[...], down[:, part]).astype(jnp.bfloat16)
        leaving.append(started(out.at[:, part], out_hbm.at[:, part], out_sem.at[n]))
    wait_all(leaving)


def expert_forward(pick, rows, own, other):
    slots, feat = rows.shape
    hidden = own[0].shape[1]
    wide = len(feature_pieces(feat))
    bf16, f32 = jnp.bfloat16, jnp.float32
    return pl.pallas_call(
        forward_kernel,
        out_shape=(
            jax.ShapeDtypeStruct((slots, feat), bf16),
            jax.ShapeDtypeStruct((slots, hidden), f32),
            jax.ShapeDtypeStruct((slots, hidden), f32),
        ),
        in_specs=[IN_SMEM] + [IN_HBM] * 7,
        out_specs=(IN_HBM,) * 3,
        scratch_shapes=[
            pltpu.VMEM((slots, feat), bf16),
            pltpu.VMEM((feat, hidden), bf16),
            pltpu.VMEM((feat, hidden), bf16),
            pltpu.VMEM((hidden, feat), bf16),
            pltpu.VMEM((slots, hidden), f32),
            pltpu.VMEM((slots, hidden), f32),
            pltpu.VMEM((slots, hidden), bf16),
            pltpu.VMEM((slots, feat), bf16),
            pltpu.SemaphoreType.DMA((wide,)),
            pltpu.SemaphoreType.DMA((wide,)),
            pltpu.SemaphoreType.DMA((wide,)),
            pltpu.SemaphoreType.DMA((wide,)),
            pltpu.SemaphoreType.DMA(()),
            pltpu.SemaphoreType.DMA(()),
            pltpu.SemaphoreType.DMA((wide,)),
        ],
        name="expert_forward",
    )(pick.reshape(1), rows, *own, *other)


def backward_kernel(
    pick_ref, rows_hbm, pre_hbm, val_hbm, gate_a, up_a, down_a, gate_b, up_b, down_b,
    out_hbm,
    rows, gate, up, down, pre, val, d_act, d_gate, d_up, out,
    in_sem, gate_sem, up_sem, down_sem, pre_sem, val_sem, out_sem,
):
    pick = pick_ref[0]
    feature_parts = feature_pieces(down.shape[1])
    line = []
    for n, part in enumerate(feature_parts):
        line.append(brought(rows_hbm.at[:, part], rows.at[:, part], in_sem.at[n]))
        line.append(fetch(pick, down_a.at[:, part], down_b.at[:, part], down.at[:, part], down_sem.at[n]))
    line.append(brought(pre_hbm, pre, pre_sem))
    line.append(brought(val_hbm, val, val_sem))
    for n, part in enumerate(feature_parts):
        line.append(fetch(pick, gate_a.at[part, :], gate_b.at[part, :], gate.at[part, :], gate_sem.at[n]))
        line.append(fetch(pick, up_a.at[part, :], up_b.at[part, :], up.at[part, :], up_sem.at[n]))
    incoming = Incoming(line, BACKWARD_AHEAD)
    for n, part in enumerate(feature_parts):
        incoming.take(2)
        partial = turned_dot(rows[:, part], down[:, part])
        d_act[...] = partial if n == 0 else d_act[...] + partial
    incoming.take(2)
    part_gate, part_up = gate_grads(d_act[...], pre[...], val[...])
    d_gate[...] = part_gate
    d_up[...] = part_up
    leaving = []
    for n, part in enumerate(feature_parts):
        incoming.take(2)
        summed = turned_dot(d_gate[...], gate[part, :]) + turned_dot(d_up[...], up[part, :])
        out[:, part] = summed.astype(jnp.bfloat16)
        leaving.append(started(out.at[:, part], out_hbm.at[:, part], out_sem.at[n]))
    wait_all(leaving)


def expert_backward(pick, rows, pre, val, own, other):
    slots, feat = rows.shape
    hidden = own[0].shape[1]
    wide = len(feature_pieces(feat))
    bf16, f32 = jnp.bfloat16, jnp.float32
    return pl.pallas_call(
        backward_kernel,
        out_shape=jax.ShapeDtypeStruct((slots, feat), bf16),
        in_specs=[IN_SMEM] + [IN_HBM] * 9,
        out_specs=IN_HBM,
        scratch_shapes=[
            pltpu.VMEM((slots, feat), bf16),
            pltpu.VMEM((feat, hidden), bf16),
            pltpu.VMEM((feat, hidden), bf16),
            pltpu.VMEM((hidden, feat), bf16),
            pltpu.VMEM((slots, hidden), f32),
            pltpu.VMEM((slots, hidden), f32),
            pltpu.VMEM((slots, hidden), f32),
            pltpu.VMEM((slots, hidden), bf16),
            pltpu.VMEM((slots, hidden), bf16),
            pltpu.VMEM((slots, feat), bf16),
            pltpu.SemaphoreType.DMA((wide,)),
            pltpu.SemaphoreType.DMA((wide,)),
            pltpu.SemaphoreType.DMA((wide,)),
            pltpu.SemaphoreType.DMA((wide,)),
            pltpu.SemaphoreType.DMA(()),
            pltpu.SemaphoreType.DMA(()),
            pltpu.SemaphoreType.DMA((wide,)),
        ],
        name="expert_backward",
    )(pick.reshape(1), rows, pre, val, *own, *other)


def joint_kernel(
    pick_ref, rows_hbm, d_act_hbm, gate_a, up_a, gate_b, up_b,
    act_hbm, out_hbm,
    rows, gate, up, d_act, pre, val, act, d_gate, d_up, out, in_sem, gate_sem, up_sem, d_act_sem, act_sem, out_sem,
):
    pick = pick_ref[0]
    feature_parts = feature_pieces(out.shape[1])
    line = []
    for n, part in enumerate(feature_parts):
        line.append(brought(rows_hbm.at[:, part], rows.at[:, part], in_sem.at[n]))
        line.append(fetch(pick, gate_a.at[part, :], gate_b.at[part, :], gate.at[part, :], gate_sem.at[n]))
        line.append(fetch(pick, up_a.at[part, :], up_b.at[part, :], up.at[part, :], up_sem.at[n]))
    line.append(brought(d_act_hbm, d_act, d_act_sem))
    incoming = Incoming(line, FORWARD_AHEAD)
    for n, part in enumerate(feature_parts):
        incoming.take(3)
        gate_part = wide_dot(rows[:, part], gate[part, :])
        up_part = wide_dot(rows[:, part], up[part, :])
        pre[...] = gate_part if n == 0 else pre[...] + gate_part
        val[...] = up_part if n == 0 else val[...] + up_part
    act[...] = (pre[...] * jax.nn.sigmoid(pre[...]) * val[...]).astype(jnp.bfloat16)
    leaving = [started(act, act_hbm, act_sem)]
    incoming.take(1)
    part_gate, part_up = gate_grads(d_act[...], pre[...], val[...])
    d_gate[...] = part_gate
    d_up[...] = part_up
    for n, part in enumerate(feature_parts):
        summed = turned_dot(d_gate[...], gate[part, :]) + turned_dot(d_up[...], up[part, :])
        out[:, part] = summed.astype(jnp.bfloat16)
        leaving.append(started(out.at[:, part], out_hbm.at[:, part], out_sem.at[n]))
    wait_all(leaving)


def expert_joint(pick, rows, d_act, own, other):
    slots, feat = rows.shape
    hidden = own[0].shape[1]
    wide = len(feature_pieces(feat))
    bf16, f32 = jnp.bfloat16, jnp.float32
    return pl.pallas_call(
        joint_kernel,
        out_shape=(
            jax.ShapeDtypeStruct((slots, hidden), bf16),
            jax.ShapeDtypeStruct((slots, feat), bf16),
        ),
        in_specs=[IN_SMEM] + [IN_HBM] * 6,
        out_specs=(IN_HBM,) * 2,
        scratch_shapes=[
            pltpu.VMEM((slots, feat), bf16),
            pltpu.VMEM((feat, hidden), bf16),
            pltpu.VMEM((feat, hidden), bf16),
            pltpu.VMEM((slots, hidden), f32),
            pltpu.VMEM((slots, hidden), f32),
            pltpu.VMEM((slots, hidden), f32),
            pltpu.VMEM((slots, hidden), bf16),
            pltpu.VMEM((slots, hidden), bf16),
            pltpu.VMEM((slots, hidden), bf16),
            pltpu.VMEM((slots, feat), bf16),
            pltpu.SemaphoreType.DMA((wide,)),
            pltpu.SemaphoreType.DMA((wide,)),
            pltpu.SemaphoreType.DMA((wide,)),
            pltpu.SemaphoreType.DMA(()),
            pltpu.SemaphoreType.DMA(()),
            pltpu.SemaphoreType.DMA((wide,)),
        ],
        name="expert_joint",
    )(pick.reshape(1), rows, d_act, *own[:2], *other[:2])


def exchange(rows):
    feat = rows.shape[1]
    peers = lax.axis_size("expert")
    blocks = rows.reshape(peers, -1, feat)
    moved = lax.all_to_all(blocks, "expert", split_axis=0, concat_axis=0, tiled=True)
    return moved.reshape(rows.shape)


def slot_matrices(route_block, gate_block, experts, capacity):
    flat_ids = route_block.reshape(-1)
    count = flat_ids.shape[0]
    onehot = flat_ids[:, None] == jnp.arange(experts, dtype=jnp.int32)[None, :]
    order = jnp.arange(count, dtype=jnp.int32)
    earlier = (order[:, None] > order[None, :]).astype(jnp.bfloat16)
    before = jnp.dot(
        earlier, onehot.astype(jnp.bfloat16), preferred_element_type=jnp.float32
    )
    position = jnp.sum(jnp.where(onehot, before, 0.0), axis=1).astype(jnp.int32)
    slots = (flat_ids * capacity + position).reshape(route_block.shape)
    places = jnp.arange(experts * capacity, dtype=jnp.int32)
    hit = slots[:, :, None] == places[None, None, :]
    picks = jnp.sum(hit.astype(jnp.float32), axis=1)
    weights = jnp.sum(jnp.where(hit, gate_block[:, :, None], 0.0), axis=1)
    return picks.astype(jnp.bfloat16), weights


def spread(picks, rows):
    return lax.dot_general(
        picks, rows, (((0,), (0,)), ((), ())), preferred_element_type=jnp.float32
    )


def gathered_sum(weights, rows):
    high = lax.reduce_precision(weights, 8, 7)
    both = jnp.concatenate([high, weights - high], axis=0).astype(jnp.bfloat16)
    parts = jnp.dot(both, rows, preferred_element_type=jnp.float32)
    half = weights.shape[0]
    return parts[:half] + parts[half:]


def inverse_rms(wide_in):
    return lax.rsqrt(jnp.mean(wide_in * wide_in, axis=1, keepdims=True) + epsilon)


def normed_rows(layer_in, gain):
    wide_in = layer_in.astype(jnp.float32)
    return (wide_in * inverse_rms(wide_in) * gain).astype(jnp.bfloat16)


def project_down(activated, down_mat):
    return jnp.dot(activated, down_mat, preferred_element_type=jnp.float32).astype(jnp.bfloat16)


def hidden_grad(d_rows, down_mat):
    return lax.dot_general(d_rows, down_mat, CONTRACT, preferred_element_type=jnp.float32)


def layer_grad(dy, layer_in, gain, picks, returned):
    wide_in = layer_in.astype(jnp.float32)
    inv_rms = inverse_rms(wide_in)
    d_norm = jnp.dot(picks, returned, preferred_element_type=jnp.float32)
    scaled = gain * d_norm
    inner = jnp.mean(wide_in * scaled, axis=1, keepdims=True)
    cubed = inv_rms * inv_rms * inv_rms
    return (dy.astype(jnp.float32) + inv_rms * scaled - wide_in * cubed * inner).astype(
        jnp.bfloat16
    )


def local(inputs, cotangent, norm_gain, routes, route_gates, w_gate, w_up, w_down):
    segment_id = lax.axis_index("segment")
    experts = lax.axis_size("expert") * w_gate.shape[1]
    micro_count, tok_rows, feat_width = inputs.shape
    capacity = min(tok_rows, 4 * tok_rows * TOP // (3 * experts))
    hidden = w_gate.shape[3]
    slots = experts * capacity
    mine = segment_id % 2
    early = segment_id < 2
    swap = [(0, 1), (1, 0), (2, 3), (3, 2)]

    def swapped(value):
        return lax.ppermute(value, "segment", swap)

    def ordered(own, other):
        low = jnp.where(mine == 0, own, other)
        high = jnp.where(mine == 0, other, own)
        return low, high

    def of_micro(value, which):
        return lax.dynamic_index_in_dim(value, which, 0, keepdims=False)

    own_mats = (w_gate[0, 0], w_up[0, 0], w_down[0, 0])
    route_low, route_high = ordered(
        of_micro(routes[0], mine), swapped(of_micro(routes[0], 1 - mine))
    )
    gate_low, gate_high = ordered(
        of_micro(route_gates[0], mine), swapped(of_micro(route_gates[0], 1 - mine))
    )
    gain_low, gain_high = ordered(norm_gain, swapped(norm_gain))
    other_mats = tuple(swapped(mat) for mat in own_mats)

    def with_mats(level, run, *values):
        return lax.cond(
            mine == level,
            lambda held: run(held, own_mats),
            lambda held: run(held, other_mats),
            values,
        )

    low_pick = mine.astype(jnp.int32)
    high_pick = 1 - low_pick

    picks_low, mix_low = slot_matrices(route_low, gate_low, experts, capacity)
    picks_high, mix_high = slot_matrices(route_high, gate_high, experts, capacity)
    scale_low = jnp.sum(mix_low, axis=0)[:, None]
    scale_high = jnp.sum(mix_high, axis=0)[:, None]

    first_in = of_micro(inputs, mine)
    last_grad = of_micro(cotangent, mine)
    source = jnp.where(early, normed_rows(first_in, gain_low), last_grad)
    picks_first = jnp.where(early, picks_low, picks_high)
    picks_first = held_back(source, picks_first, jnp.where(mine == 1, LAG_NANOS, 0))
    scale_first = jnp.where(early, 1.0, scale_high)
    arrived = exchange((scale_first * spread(picks_first, source)).astype(jnp.bfloat16))

    def send_rows(layer_in, gain, picks):
        return exchange(spread(picks, normed_rows(layer_in, gain)).astype(jnp.bfloat16))

    def send_grads(dy, picks, scale):
        return exchange((scale * spread(picks, dy)).astype(jnp.bfloat16))

    def mixed(layer_in, mix, returned):
        return (layer_in.astype(jnp.float32) + gathered_sum(mix, returned)).astype(jnp.bfloat16)

    no_rows = jnp.zeros((tok_rows, feat_width), jnp.bfloat16)
    no_hidden = jnp.zeros((slots, hidden), jnp.float32)

    def climb(got):
        out_low, pre_low, up_low = expert_forward(low_pick, got, own_mats, other_mats)
        state_low = mixed(first_in, mix_low, exchange(out_low))
        got_high = send_rows(state_low, gain_high, picks_high)
        out_high, pre_high, up_high = expert_forward(high_pick, got_high, own_mats, other_mats)
        state_high = mixed(state_low, mix_high, exchange(out_high))
        return state_low, state_high, pre_low, up_low, pre_high, up_high

    def prepare(got):
        d_act = with_mats(1, lambda held, mats: hidden_grad(held[0], mats[2]), got)
        return no_rows, no_rows, d_act, no_hidden, no_hidden, no_hidden

    state_low, state_high, kept_a, kept_b, kept_c, kept_d = lax.cond(
        early, climb, prepare, arrived
    )
    relayed = lax.ppermute(state_high, "segment", [(0, 2), (1, 3)])

    turn_gain = held_back(relayed, gain_low, jnp.where(mine == 1, TURN_LAG_NANOS, 0))
    shared_state = lax.ppermute(
        jnp.where(mine == 0, state_high, state_low), "segment", [(0, 1), (1, 0)]
    )

    def turn(held):
        layer_in, d_act, first_gain = held
        got_low = send_rows(layer_in, first_gain, picks_low)
        out_low, pre_low, up_low = expert_forward(low_pick, got_low, own_mats, other_mats)
        state = mixed(layer_in, mix_low, exchange(out_low))
        got_high = send_rows(state, gain_high, picks_high)
        activated, d_rows = expert_joint(high_pick, got_high, d_act, own_mats, other_mats)
        grad_high = layer_grad(last_grad, state, gain_high, picks_high, exchange(d_rows))
        d_got = send_grads(grad_high, picks_low, scale_low)
        d_rows_low = expert_backward(low_pick, d_got, pre_low, up_low, own_mats, other_mats)
        grad_low = layer_grad(grad_high, layer_in, gain_low, picks_low, exchange(d_rows_low))
        return state, activated, grad_high, grad_low

    def stay(held):
        return no_rows, jnp.zeros((slots, hidden), jnp.bfloat16), no_rows, no_rows

    turn_state, activated, turn_high, turn_low = lax.cond(
        early, stay, turn, (relayed, kept_a, turn_gain)
    )
    came_back = lax.ppermute(turn_low, "segment", [(2, 0), (3, 1)])

    return_picks = held_back(came_back, picks_high, jnp.where(mine == 1, RETURN_LAG_NANOS, 0))

    def descend(held):
        dy, first_picks = held
        d_got = send_grads(dy, first_picks, scale_high)
        d_rows_high = expert_backward(high_pick, d_got, kept_c, kept_d, own_mats, other_mats)
        grad_high = layer_grad(dy, state_low, gain_high, picks_high, exchange(d_rows_high))
        d_got_low = send_grads(grad_high, picks_low, scale_low)
        d_rows_low = expert_backward(low_pick, d_got_low, kept_a, kept_b, own_mats, other_mats)
        grad_low = layer_grad(grad_high, first_in, gain_low, picks_low, exchange(d_rows_low))
        return state_low, state_high, grad_low, grad_high

    def finish(held):
        out_high = with_mats(1, lambda held, mats: project_down(held[0], mats[2]), activated)
        state = mixed(turn_state, mix_high, exchange(out_high))
        return turn_state, state, turn_low, turn_high

    end_low, end_high, back_low, back_high = lax.cond(
        early, descend, finish, (came_back, return_picks)
    )
    other_grad = swapped(jnp.where(mine == 0, back_high, back_low))
    late_state = lax.ppermute(
        jnp.where(mine == 0, end_high, end_low), "segment", [(2, 3), (3, 2)]
    )
    other_state = jnp.where(early, shared_state, late_state)

    def by_micro(low, high, other):
        own = jnp.where(mine == 0, low, high)
        first = jnp.where(mine == 0, own, other)
        second = jnp.where(mine == 0, other, own)
        return jnp.stack([first, second])[None]

    return by_micro(end_low, end_high, other_state), by_micro(back_low, back_high, other_grad)


def solution(mesh):
    placed = (
        P(None, "expert", None),
        P(None, "expert", None),
        P("segment", None),
        P("segment", None, "expert", None),
        P("segment", None, "expert", None),
        P("segment", "expert", None, None),
        P("segment", "expert", None, None),
        P("segment", "expert", None, None),
    )
    return jax.shard_map(
        local,
        mesh=mesh,
        in_specs=placed,
        out_specs=(P("segment", None, "expert", None), P("segment", None, "expert", None)),
        check_vma=False,
    )
```

```python
import jax
import jax.numpy as jnp
from jax import lax
from jax.experimental import pallas as pl
from jax.experimental.pallas import tpu as pltpu
from jax.sharding import PartitionSpec as P

TOP = 6

epsilon = 1e-06

LAG_NANOS = 20000
TURN_LAG_NANOS = 4000
RETURN_LAG_NANOS = 1500
FORWARD_AHEAD = 5
FEATURE_STEP = 512
CONTRACT = (((1,), (1,)), ((), ()))
IN_HBM = pl.BlockSpec(memory_space=pl.ANY)
IN_SMEM = pl.BlockSpec(memory_space=pltpu.SMEM)
IN_VMEM = pl.BlockSpec(memory_space=pltpu.VMEM)


def late_kernel(nanos_ref, anchor_ref, value_ref, out_ref):
    pl.delay(nanos_ref[0])
    out_ref[...] = value_ref[...]


def held_back(anchor, value, nanos):
    return pl.pallas_call(
        late_kernel,
        out_shape=jax.ShapeDtypeStruct(value.shape, value.dtype),
        in_specs=[IN_SMEM, IN_HBM, IN_VMEM],
        out_specs=IN_VMEM,
        name="held_back",
    )(nanos.reshape(1), anchor, value)


def launch(pick, own, other, target, sem):
    @pl.when(pick == 0)
    def _():
        pltpu.make_async_copy(own, target, sem).start()

    @pl.when(pick != 0)
    def _():
        pltpu.make_async_copy(other, target, sem).start()


def fetch(pick, own, other, target, sem):
    def start():
        launch(pick, own, other, target, sem)
        return pltpu.make_async_copy(own, target, sem)

    return start


def brought(source, target, sem):
    return lambda: started(source, target, sem)


def started(source, target, sem):
    copy = pltpu.make_async_copy(source, target, sem)
    copy.start()
    return copy


def wait_all(copies):
    for copy in copies:
        copy.wait()


class Incoming:
    def __init__(self, starters, ahead):
        self.starters = starters
        self.ahead = ahead
        self.flying = []
        self.taken = 0
        self.launch(1 + ahead)

    def launch(self, upto):
        for start in self.starters[len(self.flying) : upto]:
            self.flying.append(start())

    def take(self, count):
        for _ in range(count):
            self.flying[self.taken].wait()
            self.taken += 1
            self.launch(self.taken + 1 + self.ahead)


def pieces(total, widths):
    parts = []
    at = 0
    for width in widths:
        size = min(width, total - at)
        if size > 0:
            parts.append(pl.ds(at, size))
            at += size
    if at < total:
        parts.append(pl.ds(at, total - at))
    return parts


def feature_pieces(total):
    return pieces(total, (512,) * (total // 512))


def arrive(source, target, sem):
    pltpu.make_async_copy(source, target, sem).wait()


def block(n):
    return pl.ds(pl.multiple_of(n * FEATURE_STEP, FEATURE_STEP), FEATURE_STEP)


def staged(count, first, later, work):
    for n in range(2):
        first(n)

    def step(n, carry):
        @pl.when(n + 2 < count)
        def _():
            first(n + 2)

        @pl.when(n + 2 >= count)
        def _():
            later(n + 2 - count)

        work(n)
        return carry

    lax.fori_loop(0, count, step, 0)


def continued(count, first, work):
    def step(n, carry):
        @pl.when(n + 2 < count)
        def _():
            first(n + 2)

        work(n)
        return carry

    lax.fori_loop(0, count, step, 0)


def wide_dot(left, right):
    return jnp.dot(left, right, preferred_element_type=jnp.float32)


def turned_dot(left, right):
    return lax.dot_general(left, right, CONTRACT, preferred_element_type=jnp.float32)


def gate_grads(d_act, gate_pre, up_val):
    sigmoid_g = jax.nn.sigmoid(gate_pre)
    d_gate = d_act * up_val * sigmoid_g * (1.0 + gate_pre * (1.0 - sigmoid_g))
    d_up = d_act * gate_pre * sigmoid_g
    return d_gate.astype(jnp.bfloat16), d_up.astype(jnp.bfloat16)


def forward_kernel(
    pick_ref, rows_hbm, gate_a, up_a, down_a, gate_b, up_b, down_b,
    out_hbm, pre_hbm, val_hbm,
    rows, gate, up, down, pre, val, act, out, in_sem, gate_sem, up_sem, down_sem, pre_sem, val_sem, out_sem,
):
    pick = pick_ref[0]
    feature_parts = feature_pieces(down.shape[1])
    line = []
    for n, part in enumerate(feature_parts):
        line.append(brought(rows_hbm.at[:, part], rows.at[:, part], in_sem.at[n]))
        line.append(fetch(pick, gate_a.at[part, :], gate_b.at[part, :], gate.at[part, :], gate_sem.at[n]))
        line.append(fetch(pick, up_a.at[part, :], up_b.at[part, :], up.at[part, :], up_sem.at[n]))
    for n, part in enumerate(feature_parts):
        line.append(fetch(pick, down_a.at[:, part], down_b.at[:, part], down.at[:, part], down_sem.at[n]))
    incoming = Incoming(line, FORWARD_AHEAD)
    for n, part in enumerate(feature_parts):
        incoming.take(3)
        gate_part = wide_dot(rows[:, part], gate[part, :])
        up_part = wide_dot(rows[:, part], up[part, :])
        pre[...] = gate_part if n == 0 else pre[...] + gate_part
        val[...] = up_part if n == 0 else val[...] + up_part
    leaving = [started(pre, pre_hbm, pre_sem), started(val, val_hbm, val_sem)]
    act[...] = (pre[...] * jax.nn.sigmoid(pre[...]) * val[...]).astype(jnp.bfloat16)
    for n, part in enumerate(feature_parts):
        incoming.take(1)
        out[:, part] = wide_dot(act[...], down[:, part]).astype(jnp.bfloat16)
        leaving.append(started(out.at[:, part], out_hbm.at[:, part], out_sem.at[n]))
    wait_all(leaving)


def expert_forward(pick, rows, own, other):
    slots, feat = rows.shape
    hidden = own[0].shape[1]
    wide = len(feature_pieces(feat))
    bf16, f32 = jnp.bfloat16, jnp.float32
    return pl.pallas_call(
        forward_kernel,
        out_shape=(
            jax.ShapeDtypeStruct((slots, feat), bf16),
            jax.ShapeDtypeStruct((slots, hidden), f32),
            jax.ShapeDtypeStruct((slots, hidden), f32),
        ),
        in_specs=[IN_SMEM] + [IN_HBM] * 7,
        out_specs=(IN_HBM,) * 3,
        scratch_shapes=[
            pltpu.VMEM((slots, feat), bf16),
            pltpu.VMEM((feat, hidden), bf16),
            pltpu.VMEM((feat, hidden), bf16),
            pltpu.VMEM((hidden, feat), bf16),
            pltpu.VMEM((slots, hidden), f32),
            pltpu.VMEM((slots, hidden), f32),
            pltpu.VMEM((slots, hidden), bf16),
            pltpu.VMEM((slots, feat), bf16),
            pltpu.SemaphoreType.DMA((wide,)),
            pltpu.SemaphoreType.DMA((wide,)),
            pltpu.SemaphoreType.DMA((wide,)),
            pltpu.SemaphoreType.DMA((wide,)),
            pltpu.SemaphoreType.DMA(()),
            pltpu.SemaphoreType.DMA(()),
            pltpu.SemaphoreType.DMA((wide,)),
        ],
        name="expert_forward",
    )(pick.reshape(1), rows, *own, *other)


def backward_kernel(
    pick_ref, rows_hbm, pre_hbm, val_hbm, gate_a, up_a, down_a, gate_b, up_b, down_b,
    out_hbm,
    rows, gate, up, down, pre, val, d_act, d_gate, d_up, out,
    in_sem, gate_sem, up_sem, down_sem, pre_sem, val_sem, out_sem,
):
    pick = pick_ref[0]
    count = down.shape[1] // FEATURE_STEP

    def first(n):
        part = block(n)
        started(rows_hbm.at[:, part], rows.at[:, part], in_sem.at[n])
        launch(pick, down_a.at[:, part], down_b.at[:, part], down.at[:, part], down_sem.at[n])

    def second(n):
        part = block(n)
        launch(pick, gate_a.at[part, :], gate_b.at[part, :], gate.at[part, :], gate_sem.at[n])
        launch(pick, up_a.at[part, :], up_b.at[part, :], up.at[part, :], up_sem.at[n])

    def widen(n):
        part = block(n)

        @pl.when(n == 1)
        def _():
            started(pre_hbm, pre, pre_sem)
            started(val_hbm, val, val_sem)

        arrive(rows_hbm.at[:, part], rows.at[:, part], in_sem.at[n])
        arrive(down_a.at[:, part], down.at[:, part], down_sem.at[n])
        d_act[...] += turned_dot(rows[:, part], down[:, part])

    def narrow(n):
        part = block(n)
        arrive(gate_a.at[part, :], gate.at[part, :], gate_sem.at[n])
        arrive(up_a.at[part, :], up.at[part, :], up_sem.at[n])
        summed = turned_dot(d_gate[...], gate[part, :]) + turned_dot(d_up[...], up[part, :])
        out[:, part] = summed.astype(jnp.bfloat16)
        started(out.at[:, part], out_hbm.at[:, part], out_sem.at[n])

    d_act[...] = jnp.zeros_like(d_act)
    staged(count, first, second, widen)
    arrive(pre_hbm, pre, pre_sem)
    arrive(val_hbm, val, val_sem)
    part_gate, part_up = gate_grads(d_act[...], pre[...], val[...])
    d_gate[...] = part_gate
    d_up[...] = part_up
    continued(count, second, narrow)
    for n in range(count):
        arrive(out.at[:, block(n)], out_hbm.at[:, block(n)], out_sem.at[n])


def expert_backward(pick, rows, pre, val, own, other):
    slots, feat = rows.shape
    hidden = own[0].shape[1]
    wide = len(feature_pieces(feat))
    bf16, f32 = jnp.bfloat16, jnp.float32
    return pl.pallas_call(
        backward_kernel,
        out_shape=jax.ShapeDtypeStruct((slots, feat), bf16),
        in_specs=[IN_SMEM] + [IN_HBM] * 9,
        out_specs=IN_HBM,
        scratch_shapes=[
            pltpu.VMEM((slots, feat), bf16),
            pltpu.VMEM((feat, hidden), bf16),
            pltpu.VMEM((feat, hidden), bf16),
            pltpu.VMEM((hidden, feat), bf16),
            pltpu.VMEM((slots, hidden), f32),
            pltpu.VMEM((slots, hidden), f32),
            pltpu.VMEM((slots, hidden), f32),
            pltpu.VMEM((slots, hidden), bf16),
            pltpu.VMEM((slots, hidden), bf16),
            pltpu.VMEM((slots, feat), bf16),
            pltpu.SemaphoreType.DMA((wide,)),
            pltpu.SemaphoreType.DMA((wide,)),
            pltpu.SemaphoreType.DMA((wide,)),
            pltpu.SemaphoreType.DMA((wide,)),
            pltpu.SemaphoreType.DMA(()),
            pltpu.SemaphoreType.DMA(()),
            pltpu.SemaphoreType.DMA((wide,)),
        ],
        name="expert_backward",
    )(pick.reshape(1), rows, pre, val, *own, *other)


def joint_kernel(
    pick_ref, rows_hbm, d_act_hbm, gate_a, up_a, gate_b, up_b,
    act_hbm, out_hbm,
    rows, gate, up, d_act, pre, val, act, d_gate, d_up, out, in_sem, gate_sem, up_sem, d_act_sem, act_sem, out_sem,
):
    pick = pick_ref[0]
    feature_parts = feature_pieces(out.shape[1])
    line = []
    for n, part in enumerate(feature_parts):
        line.append(brought(rows_hbm.at[:, part], rows.at[:, part], in_sem.at[n]))
        line.append(fetch(pick, gate_a.at[part, :], gate_b.at[part, :], gate.at[part, :], gate_sem.at[n]))
        line.append(fetch(pick, up_a.at[part, :], up_b.at[part, :], up.at[part, :], up_sem.at[n]))
    line.append(brought(d_act_hbm, d_act, d_act_sem))
    incoming = Incoming(line, FORWARD_AHEAD)
    for n, part in enumerate(feature_parts):
        incoming.take(3)
        gate_part = wide_dot(rows[:, part], gate[part, :])
        up_part = wide_dot(rows[:, part], up[part, :])
        pre[...] = gate_part if n == 0 else pre[...] + gate_part
        val[...] = up_part if n == 0 else val[...] + up_part
    act[...] = (pre[...] * jax.nn.sigmoid(pre[...]) * val[...]).astype(jnp.bfloat16)
    leaving = [started(act, act_hbm, act_sem)]
    incoming.take(1)
    part_gate, part_up = gate_grads(d_act[...], pre[...], val[...])
    d_gate[...] = part_gate
    d_up[...] = part_up
    for n, part in enumerate(feature_parts):
        summed = turned_dot(d_gate[...], gate[part, :]) + turned_dot(d_up[...], up[part, :])
        out[:, part] = summed.astype(jnp.bfloat16)
        leaving.append(started(out.at[:, part], out_hbm.at[:, part], out_sem.at[n]))
    wait_all(leaving)


def expert_joint(pick, rows, d_act, own, other):
    slots, feat = rows.shape
    hidden = own[0].shape[1]
    wide = len(feature_pieces(feat))
    bf16, f32 = jnp.bfloat16, jnp.float32
    return pl.pallas_call(
        joint_kernel,
        out_shape=(
            jax.ShapeDtypeStruct((slots, hidden), bf16),
            jax.ShapeDtypeStruct((slots, feat), bf16),
        ),
        in_specs=[IN_SMEM] + [IN_HBM] * 6,
        out_specs=(IN_HBM,) * 2,
        scratch_shapes=[
            pltpu.VMEM((slots, feat), bf16),
            pltpu.VMEM((feat, hidden), bf16),
            pltpu.VMEM((feat, hidden), bf16),
            pltpu.VMEM((slots, hidden), f32),
            pltpu.VMEM((slots, hidden), f32),
            pltpu.VMEM((slots, hidden), f32),
            pltpu.VMEM((slots, hidden), bf16),
            pltpu.VMEM((slots, hidden), bf16),
            pltpu.VMEM((slots, hidden), bf16),
            pltpu.VMEM((slots, feat), bf16),
            pltpu.SemaphoreType.DMA((wide,)),
            pltpu.SemaphoreType.DMA((wide,)),
            pltpu.SemaphoreType.DMA((wide,)),
            pltpu.SemaphoreType.DMA(()),
            pltpu.SemaphoreType.DMA(()),
            pltpu.SemaphoreType.DMA((wide,)),
        ],
        name="expert_joint",
    )(pick.reshape(1), rows, d_act, *own[:2], *other[:2])


def exchange(rows):
    feat = rows.shape[1]
    peers = lax.axis_size("expert")
    blocks = rows.reshape(peers, -1, feat)
    moved = lax.all_to_all(blocks, "expert", split_axis=0, concat_axis=0, tiled=True)
    return moved.reshape(rows.shape)


def slot_matrices(route_block, gate_block, experts, capacity):
    flat_ids = route_block.reshape(-1)
    count = flat_ids.shape[0]
    onehot = flat_ids[:, None] == jnp.arange(experts, dtype=jnp.int32)[None, :]
    order = jnp.arange(count, dtype=jnp.int32)
    earlier = (order[:, None] > order[None, :]).astype(jnp.bfloat16)
    before = jnp.dot(
        earlier, onehot.astype(jnp.bfloat16), preferred_element_type=jnp.float32
    )
    position = jnp.sum(jnp.where(onehot, before, 0.0), axis=1).astype(jnp.int32)
    slots = (flat_ids * capacity + position).reshape(route_block.shape)
    places = jnp.arange(experts * capacity, dtype=jnp.int32)
    hit = slots[:, :, None] == places[None, None, :]
    picks = jnp.sum(hit.astype(jnp.float32), axis=1)
    weights = jnp.sum(jnp.where(hit, gate_block[:, :, None], 0.0), axis=1)
    return picks.astype(jnp.bfloat16), weights


def spread(picks, rows):
    return lax.dot_general(
        picks, rows, (((0,), (0,)), ((), ())), preferred_element_type=jnp.float32
    )


def gathered_sum(weights, rows):
    high = lax.reduce_precision(weights, 8, 7)
    both = jnp.concatenate([high, weights - high], axis=0).astype(jnp.bfloat16)
    parts = jnp.dot(both, rows, preferred_element_type=jnp.float32)
    half = weights.shape[0]
    return parts[:half] + parts[half:]


def inverse_rms(wide_in):
    return lax.rsqrt(jnp.mean(wide_in * wide_in, axis=1, keepdims=True) + epsilon)


def normed_rows(layer_in, gain):
    wide_in = layer_in.astype(jnp.float32)
    return (wide_in * inverse_rms(wide_in) * gain).astype(jnp.bfloat16)


def project_down(activated, down_mat):
    return jnp.dot(activated, down_mat, preferred_element_type=jnp.float32).astype(jnp.bfloat16)


def hidden_grad(d_rows, down_mat):
    return lax.dot_general(d_rows, down_mat, CONTRACT, preferred_element_type=jnp.float32)


def layer_grad(dy, layer_in, gain, picks, returned):
    wide_in = layer_in.astype(jnp.float32)
    inv_rms = inverse_rms(wide_in)
    d_norm = jnp.dot(picks, returned, preferred_element_type=jnp.float32)
    scaled = gain * d_norm
    inner = jnp.mean(wide_in * scaled, axis=1, keepdims=True)
    cubed = inv_rms * inv_rms * inv_rms
    return (dy.astype(jnp.float32) + inv_rms * scaled - wide_in * cubed * inner).astype(
        jnp.bfloat16
    )


def local(inputs, cotangent, norm_gain, routes, route_gates, w_gate, w_up, w_down):
    segment_id = lax.axis_index("segment")
    experts = lax.axis_size("expert") * w_gate.shape[1]
    micro_count, tok_rows, feat_width = inputs.shape
    capacity = min(tok_rows, 4 * tok_rows * TOP // (3 * experts))
    hidden = w_gate.shape[3]
    slots = experts * capacity
    mine = segment_id % 2
    early = segment_id < 2
    swap = [(0, 1), (1, 0), (2, 3), (3, 2)]

    def swapped(value):
        return lax.ppermute(value, "segment", swap)

    def ordered(own, other):
        low = jnp.where(mine == 0, own, other)
        high = jnp.where(mine == 0, other, own)
        return low, high

    def of_micro(value, which):
        return lax.dynamic_index_in_dim(value, which, 0, keepdims=False)

    own_mats = (w_gate[0, 0], w_up[0, 0], w_down[0, 0])
    route_low, route_high = ordered(
        of_micro(routes[0], mine), swapped(of_micro(routes[0], 1 - mine))
    )
    gate_low, gate_high = ordered(
        of_micro(route_gates[0], mine), swapped(of_micro(route_gates[0], 1 - mine))
    )
    gain_low, gain_high = ordered(norm_gain, swapped(norm_gain))
    other_mats = tuple(swapped(mat) for mat in own_mats)

    def with_mats(level, run, *values):
        return lax.cond(
            mine == level,
            lambda held: run(held, own_mats),
            lambda held: run(held, other_mats),
            values,
        )

    low_pick = mine.astype(jnp.int32)
    high_pick = 1 - low_pick

    picks_first, mix_first = slot_matrices(
        jnp.where(early, route_low, route_high),
        jnp.where(early, gate_low, gate_high),
        experts,
        capacity,
    )
    scale_first = jnp.where(early, 1.0, jnp.sum(mix_first, axis=0))[:, None]
    first_in = of_micro(inputs, mine)
    last_grad = of_micro(cotangent, mine)
    source = jnp.where(early, normed_rows(first_in, gain_low), last_grad)
    picks_held = held_back(source, picks_first, jnp.where(mine == 1, LAG_NANOS, 0))
    outgoing = (scale_first * spread(picks_held, source)).astype(jnp.bfloat16)
    outgoing, route_next, gate_next = lax.optimization_barrier(
        (
            outgoing,
            jnp.where(early, route_high, route_low),
            jnp.where(early, gate_high, gate_low),
        )
    )
    arrived = exchange(outgoing)
    picks_next, mix_next = slot_matrices(route_next, gate_next, experts, capacity)
    picks_low = jnp.where(early, picks_first, picks_next)
    picks_high = jnp.where(early, picks_next, picks_first)
    mix_low = jnp.where(early, mix_first, mix_next)
    mix_high = jnp.where(early, mix_next, mix_first)
    scale_low = jnp.sum(mix_low, axis=0)[:, None]
    scale_high = jnp.sum(mix_high, axis=0)[:, None]

    def send_rows(layer_in, gain, picks):
        return exchange(spread(picks, normed_rows(layer_in, gain)).astype(jnp.bfloat16))

    def send_grads(dy, picks, scale):
        return exchange((scale * spread(picks, dy)).astype(jnp.bfloat16))

    def mixed(layer_in, mix, returned):
        return (layer_in.astype(jnp.float32) + gathered_sum(mix, returned)).astype(jnp.bfloat16)

    no_rows = jnp.zeros((tok_rows, feat_width), jnp.bfloat16)
    no_hidden = jnp.zeros((slots, hidden), jnp.float32)

    def climb(got):
        out_low, pre_low, up_low = expert_forward(low_pick, got, own_mats, other_mats)
        state_low = mixed(first_in, mix_low, exchange(out_low))
        got_high = send_rows(state_low, gain_high, picks_high)
        out_high, pre_high, up_high = expert_forward(high_pick, got_high, own_mats, other_mats)
        state_high = mixed(state_low, mix_high, exchange(out_high))
        return state_low, state_high, pre_low, up_low, pre_high, up_high

    def prepare(got):
        d_act = with_mats(1, lambda held, mats: hidden_grad(held[0], mats[2]), got)
        return no_rows, no_rows, d_act, no_hidden, no_hidden, no_hidden

    state_low, state_high, kept_a, kept_b, kept_c, kept_d = lax.cond(
        early, climb, prepare, arrived
    )
    relayed = lax.ppermute(state_high, "segment", [(0, 2), (1, 3)])

    turn_gain = held_back(relayed, gain_low, jnp.where(mine == 1, TURN_LAG_NANOS, 0))

    def turn(held):
        layer_in, d_act, first_gain = held
        got_low = send_rows(layer_in, first_gain, picks_low)
        out_low, pre_low, up_low = expert_forward(low_pick, got_low, own_mats, other_mats)
        state = mixed(layer_in, mix_low, exchange(out_low))
        got_high = send_rows(state, gain_high, picks_high)
        activated, d_rows = expert_joint(high_pick, got_high, d_act, own_mats, other_mats)
        grad_high = layer_grad(last_grad, state, gain_high, picks_high, exchange(d_rows))
        d_got = send_grads(grad_high, picks_low, scale_low)
        d_rows_low = expert_backward(low_pick, d_got, pre_low, up_low, own_mats, other_mats)
        grad_low = layer_grad(grad_high, layer_in, gain_low, picks_low, exchange(d_rows_low))
        return state, activated, grad_high, grad_low

    def stay(held):
        return no_rows, jnp.zeros((slots, hidden), jnp.bfloat16), no_rows, no_rows

    turn_state, activated, turn_high, turn_low = lax.cond(
        early, stay, turn, (relayed, kept_a, turn_gain)
    )
    came_back = lax.ppermute(turn_low, "segment", [(2, 0), (3, 1)])

    return_picks = held_back(came_back, picks_high, jnp.where(mine == 1, RETURN_LAG_NANOS, 0))

    def descend(held):
        dy, first_picks = held
        d_got = send_grads(dy, first_picks, scale_high)
        d_rows_high = expert_backward(high_pick, d_got, kept_c, kept_d, own_mats, other_mats)
        grad_high = layer_grad(dy, state_low, gain_high, picks_high, exchange(d_rows_high))
        d_got_low = send_grads(grad_high, picks_low, scale_low)
        d_rows_low = expert_backward(low_pick, d_got_low, kept_a, kept_b, own_mats, other_mats)
        grad_low = layer_grad(grad_high, first_in, gain_low, picks_low, exchange(d_rows_low))
        return state_low, state_high, grad_low, grad_high

    def finish(held):
        out_high = with_mats(1, lambda held, mats: project_down(held[0], mats[2]), activated)
        state = mixed(turn_state, mix_high, exchange(out_high))
        return turn_state, state, turn_low, turn_high

    end_low, end_high, back_low, back_high = lax.cond(
        early, descend, finish, (came_back, return_picks)
    )
    low = jnp.stack([end_low, back_low])
    high = jnp.stack([end_high, back_high])
    other = swapped(jnp.where(mine == 0, high, low))
    own = jnp.where(mine == 0, low, high)
    is_mine = jnp.arange(micro_count)[:, None, None] == mine
    all_states = jnp.where(is_mine, own[0][None], other[0][None])[None]
    all_grads = jnp.where(is_mine, own[1][None], other[1][None])[None]
    return all_states, all_grads


def solution(mesh):
    placed = (
        P(None, "expert", None),
        P(None, "expert", None),
        P("segment", None),
        P("segment", None, "expert", None),
        P("segment", None, "expert", None),
        P("segment", "expert", None, None),
        P("segment", "expert", None, None),
        P("segment", "expert", None, None),
    )
    return jax.shard_map(
        local,
        mesh=mesh,
        in_specs=placed,
        out_specs=(P("segment", None, "expert", None), P("segment", None, "expert", None)),
        check_vma=False,
    )
```
